256 devices in a mesh: lat: 4 (over y_lo, core), lon: 64 (over z, x, y_hi).
Axes of the slice: x: 4, y: 4 (y_hi: 2, y_lo: 2; y = y_hi * 2 + y_lo), z: 8, core: 2. Of those that a mesh axis runs over, the one named last changes fastest.
Arguments:
- residual: bfloat16 [128, 1024, 128], P('lat', 'lon'), may hold values from -6 to 6
- noise_weights: float32 [128, 1024], P('lat', 'lon'), may hold values from 0.5 to 4
- kernel: bfloat16 [4, 1, 2048, 2048], P(None, None, 'lat'), may hold values from -0.0625 to 0.0625
Outputs:
- gradient: float32 [1, 128, 1024, 128], P(None, 'lat', 'lon')
The draws below stay inside these ranges and needn't reach their ends.
All inputs are finite; a program needn't handle non-finite values.
Results may differ from the reference program's by a relative error of at most 0.0029.
Values may be sent and summed in bfloat16 or wider, within the bound.
No kernel may reach another device: no remote copies, remote signals or barrier semaphores. Data moves between devices by JAX's collectives and lax.ppermute only.
A program may use at most 64 MiB of HBM per device.

```python
import math
import jax
import jax.numpy as jnp

LON_DEV = 16
PROBES = 128
LAYERS = 1
OFFSETS = 4
NY = 128
NX = 1024
CELLS = 2048
N_LON = 64


def block_levels(stream_key, shape, split, least, top_value):
    loudness = 1.0
    for position, blocks in split:
        heights = jax.random.uniform(jax.random.fold_in(jax.random.fold_in(stream_key, 6), position), (blocks,), jnp.float32, least / len(split), top_value / len(split))
        loudness = loudness * jnp.repeat(jnp.exp(heights), shape[position] // blocks).reshape((-1,) + (1,) * (len(shape) - 1 - position))
    return loudness


def gaussian(stream_key, dims, scale, reach, cuts=(), kind=jnp.bfloat16):
    entries = jax.random.normal(stream_key, dims, jnp.float32) * scale
    if len(cuts) > 0:
        entries = block_levels(stream_key, dims, cuts, -0.22, 0.18) * entries
    return jnp.clip(entries, min=-reach, max=reach).astype(kind)


def setup_inputs(seed: int = 0) -> dict:
    key_list = jax.random.split(jax.random.key(seed), 4)
    residual = gaussian(key_list[0], (NY, NX, PROBES), 1.0, 6.0, ((0, 4), (1, 64)))
    noise_weights = jnp.clip(jnp.exp(math.log(4.0) - 2.0794415 * jax.random.uniform(key_list[1], (NY, NX), jnp.float32) ** block_levels(key_list[1], (NY, NX), ((0, 4), (1, 64)), -0.2, 0.2)), 0.5, 4.0)
    kernel = gaussian(key_list[2], (OFFSETS, LAYERS, CELLS, CELLS), (OFFSETS * CELLS) ** -0.5, 0.0625, ((2, 4),))
    return {"residual": residual, "noise_weights": noise_weights, "kernel": kernel}


def reference(residual, noise_weights, kernel):
    weighted = (noise_weights[:, :, None] * residual.astype(jnp.float32)).astype(jnp.bfloat16)
    blocks = weighted.reshape(NY, N_LON, LON_DEV, PROBES).transpose(1, 0, 2, 3)
    blocks = blocks.reshape(N_LON, NY * LON_DEV, PROBES).astype(jnp.float32)
    summed = jnp.zeros((N_LON, LAYERS, NY * LON_DEV, PROBES), jnp.float32)
    for offset in range(OFFSETS):
        shifted = jnp.roll(blocks, offset, axis=0)
        summed = summed + jnp.einsum("lqc,jqp->jlcp", kernel[offset].astype(jnp.float32), shifted)
    summed = summed.reshape(N_LON, LAYERS, NY, LON_DEV, PROBES).transpose(1, 2, 0, 3, 4)
    return summed.reshape(LAYERS, NY, NX, PROBES)
```

```python
import jax
import jax.numpy as jnp
from jax import lax
from jax.sharding import PartitionSpec as P


def eastward(value, by):
    length = lax.axis_size("lon")
    return lax.ppermute(value, "lon", [(i, (i + by) % length) for i in range(length)])


def swapped(value, mask):
    length = lax.axis_size("lat")
    return lax.ppermute(value, "lat", [(i, i ^ mask) for i in range(length)])


def per_device(residual, noise_weights, kernel):
    offsets = kernel.shape[0]
    rows, columns, probes = residual.shape
    cells = rows * columns
    weighted = (noise_weights[:, :, None] * residual.astype(jnp.float32)).astype(jnp.bfloat16)
    weighted = weighted.reshape(cells, probes)
    halo = [weighted] + [eastward(weighted, by) for by in range(1, offsets)]
    partial = sum(
        jnp.einsum("qc,qp->cp", kernel[by, 0], halo[by], preferred_element_type=jnp.float32)
        for by in range(offsets)
    )
    band = lax.axis_index("lat")
    total = lax.dynamic_slice_in_dim(partial, band * cells, cells)
    for mask in (3, 2, 1):
        other = lax.dynamic_slice_in_dim(partial, (band ^ mask) * cells, cells)
        total = total + swapped(other.astype(jnp.bfloat16), mask).astype(jnp.float32)
    return total.reshape(1, rows, columns, probes)


def solution(mesh):
    return jax.shard_map(
        per_device,
        mesh=mesh,
        in_specs=(P("lat", "lon", None), P("lat", "lon"), P(None, None, "lat", None)),
        out_specs=P(None, "lat", "lon", None),
        check_vma=False,
    )
```

```python
import functools

import jax
import jax.numpy as jnp
from jax import lax
from jax.experimental import pallas as pl
from jax.experimental.pallas import tpu as pltpu
from jax.sharding import PartitionSpec as P


VMEM = pl.BlockSpec(memory_space=pltpu.VMEM)
HBM = pl.BlockSpec(memory_space=pltpu.HBM)


def in_hbm(value):
    return pltpu.with_memory_space_constraint(value, pltpu.HBM)


def eastward(value, by):
    length = lax.axis_size("lon")
    return lax.ppermute(value, "lon", [(i, (i + by) % length) for i in range(length)])


def swapped(value, mask):
    length = lax.axis_size("lat")
    return lax.ppermute(value, "lat", [(i, i ^ mask) for i in range(length)])


def call(body, outs, in_specs, scratch, flops, nbytes, limit):
    return pl.pallas_call(
        body,
        out_shape=outs,
        in_specs=in_specs,
        out_specs=jax.tree.map(lambda _: VMEM, outs),
        scratch_shapes=scratch,
        cost_estimate=pl.CostEstimate(flops=flops, bytes_accessed=nbytes, transcendentals=0),
        compiler_params=pltpu.CompilerParams(vmem_limit_bytes=limit),
    )


def weigh_body(residual, noise, out, data, weights, sems):
    pieces, rows = data.shape[0], data.shape[1]
    first = pltpu.make_async_copy(noise, weights, sems.at[pieces])
    first.start()
    copies = [
        pltpu.make_async_copy(residual.at[pl.ds(i * rows, rows)], data.at[i], sems.at[i])
        for i in range(pieces)
    ]
    for copy in copies:
        copy.start()
    first.wait()
    cells = rows * data.shape[2]
    for i, copy in enumerate(copies):
        copy.wait()
        part = [
            weights[:, i * rows + y : i * rows + y + 1] * data[i, y].astype(jnp.float32)
            for y in range(rows)
        ]
        out[:, i * cells : (i + 1) * cells] = jnp.concatenate(part, axis=0).T.astype(out.dtype)


def first_body(weighted, panels, acc):
    cells = weighted.shape[1]
    for k in range(panels.shape[3] // cells):
        acc[:, k * cells : (k + 1) * cells] = jnp.dot(
            weighted[...],
            panels[0, 0, :, k * cells : (k + 1) * cells],
            preferred_element_type=jnp.float32,
        )


def band_sum(halo, panels, acc, band, cells):
    where = pl.ds(pl.multiple_of(band * cells, cells), cells)
    total = acc[:, where]
    for d, h in enumerate(halo):
        total += jnp.dot(h[...], panels[d + 1, 0, :, where], preferred_element_type=jnp.float32)
    return total


def partner_body(h1, h2, h3, panels, acc, out):
    core = lax.axis_index("lat") % 2
    cells = h1.shape[1]
    for chip in range(2):
        out[chip] = band_sum((h1, h2, h3), panels, acc, 2 * chip + 1 - core, cells).astype(out.dtype)


def own_body(h1, h2, h3, panels, acc, out):
    core = lax.axis_index("lat") % 2
    cells = h1.shape[1]
    for chip in range(2):
        out[chip] = band_sum((h1, h2, h3), panels, acc, 2 * chip + core, cells)


def pack_body(mine, other, out):
    far = 1 - lax.axis_index("lat") // 2
    out[...] = (mine[far] + other[far].astype(jnp.float32)).astype(out.dtype)


def final_body(mine, other, third, out):
    near = lax.axis_index("lat") // 2
    total = mine[near] + other[near].astype(jnp.float32) + third[...].astype(jnp.float32)
    out[...] = total.T


def per_device(residual, noise_weights, kernel):
    rows, columns, probes = residual.shape
    cells = rows * columns
    every = kernel.shape[3]
    f32, bf16 = jnp.float32, jnp.bfloat16
    shape = jax.ShapeDtypeStruct
    MB = 1 << 20

    pieces = 4
    weighted = call(
        weigh_body,
        shape((probes, cells), bf16),
        [HBM, HBM],
        [
            pltpu.VMEM((pieces, rows // pieces, columns, probes), bf16),
            pltpu.VMEM((columns, rows), f32),
            pltpu.SemaphoreType.DMA((pieces + 1,)),
        ],
        0,
        MB // 4,
        16 * MB,
    )(in_hbm(residual), in_hbm(noise_weights.T))
    h3, h1, h2 = [eastward(weighted, by) for by in (3, 1, 2)]
    flops = 2 * probes * cells * every
    acc = call(first_body, shape((probes, every), f32), [VMEM] * 2, [], flops, 3 * MB, 16 * MB)(
        weighted, kernel
    )
    flops = 3 * probes * cells * every
    away = call(partner_body, shape((2, probes, cells), bf16), [VMEM] * 5, [], flops, 4 * MB, 16 * MB)(
        h1, h2, h3, kernel, acc
    )
    other = swapped(away, 1)
    mine = call(own_body, shape((2, probes, cells), f32), [VMEM] * 5, [], flops, 4 * MB, 16 * MB)(
        h1, h2, h3, kernel, acc
    )
    packed = call(pack_body, shape((probes, cells), bf16), [VMEM] * 2, [], 0, MB, 4 * MB)(mine, other)
    third = swapped(packed, 2)
    total = call(final_body, shape((cells, probes), f32), [VMEM] * 3, [], 0, MB, 4 * MB)(mine, other, third)
    return total.reshape(1, rows, columns, probes)


def solution(mesh):
    return jax.shard_map(
        per_device,
        mesh=mesh,
        in_specs=(P("lat", "lon", None), P("lat", "lon"), P(None, None, "lat", None)),
        out_specs=P(None, "lat", "lon", None),
        check_vma=False,
    )
```

```python
import functools

import jax
import jax.numpy as jnp
from jax import lax
from jax.experimental import pallas as pl
from jax.experimental.pallas import tpu as pltpu
from jax.sharding import PartitionSpec as P


VMEM = pl.BlockSpec(memory_space=pltpu.VMEM)
HBM = pl.BlockSpec(memory_space=pltpu.HBM)


def in_hbm(value):
    return pltpu.with_memory_space_constraint(value, pltpu.HBM)


def eastward(value, by):
    length = lax.axis_size("lon")
    return lax.ppermute(value, "lon", [(i, (i + by) % length) for i in range(length)])


def swapped(value, mask):
    length = lax.axis_size("lat")
    return lax.ppermute(value, "lat", [(i, i ^ mask) for i in range(length)])


def call(body, outs, in_specs, scratch, flops, nbytes, limit):
    return pl.pallas_call(
        body,
        out_shape=outs,
        in_specs=in_specs,
        out_specs=jax.tree.map(lambda _: VMEM, outs),
        scratch_shapes=scratch,
        cost_estimate=pl.CostEstimate(flops=flops, bytes_accessed=nbytes, transcendentals=0),
        compiler_params=pltpu.CompilerParams(vmem_limit_bytes=limit),
    )


def weigh_body(residual, noise, out, data, weights, sems):
    pieces, rows = data.shape[0], data.shape[1]
    first = pltpu.make_async_copy(noise, weights, sems.at[pieces])
    first.start()
    copies = [
        pltpu.make_async_copy(residual.at[pl.ds(i * rows, rows)], data.at[i], sems.at[i])
        for i in range(pieces)
    ]
    for copy in copies:
        copy.start()
    first.wait()
    cells = rows * data.shape[2]
    for i, copy in enumerate(copies):
        copy.wait()
        part = [
            weights[:, i * rows + y : i * rows + y + 1] * data[i, y].astype(jnp.float32)
            for y in range(rows)
        ]
        out[:, i * cells : (i + 1) * cells] = jnp.concatenate(part, axis=0).T.astype(out.dtype)


def first_body(weighted, panels, acc, own, sems):
    cells = weighted.shape[1]
    depth = cells // sems.shape[0]
    copies = [
        pltpu.make_async_copy(
            panels.at[0, 0, pl.ds(i * depth, depth)], own.at[pl.ds(i * depth, depth)], sems.at[i]
        )
        for i in range(sems.shape[0])
    ]
    for copy in copies:
        copy.start()
    for copy in copies:
        copy.wait()
    for k in range(panels.shape[3] // cells):
        where = slice(k * cells, (k + 1) * cells)
        acc[:, where] = jnp.dot(weighted[...], own[:, where], preferred_element_type=jnp.float32)


def band_sum(halo, panels, acc, band, cells):
    where = pl.ds(pl.multiple_of(band * cells, cells), cells)
    total = acc[:, where]
    for d, h in enumerate(halo):
        total += jnp.dot(h[...], panels[d + 1, 0, :, where], preferred_element_type=jnp.float32)
    return total


def far_body(h2, h3, h1, panels, acc, out):
    band = 3 - lax.axis_index("lat")
    out[...] = band_sum((h1, h2, h3), panels, acc, band, h1.shape[1]).astype(out.dtype)


def rest_body(h2, h3, h1, panels, acc, near, mine):
    band = lax.axis_index("lat")
    partner = band + 1 - 2 * (band % 2)
    halo, cells = (h1, h2, h3), h1.shape[1]
    near[...] = band_sum(halo, panels, acc, partner, cells).astype(near.dtype)
    mine[0] = band_sum(halo, panels, acc, 3 - partner, cells)
    mine[1] = band_sum(halo, panels, acc, band, cells)


def pack_body(mine, other, out):
    out[...] = (mine[0] + other[...].astype(jnp.float32)).astype(out.dtype)


def final_body(mine, other, third, out):
    total = mine[1] + other[...].astype(jnp.float32) + third[...].astype(jnp.float32)
    out[...] = total.T


def per_device(residual, noise_weights, kernel):
    rows, columns, probes = residual.shape
    cells = rows * columns
    every = kernel.shape[3]
    f32, bf16 = jnp.float32, jnp.bfloat16
    shape = jax.ShapeDtypeStruct
    MB = 1 << 20

    pieces = 4
    weighted = call(
        weigh_body,
        pltpu.VMEM((probes, cells), bf16),
        [HBM, HBM],
        [
            pltpu.VMEM((pieces, rows // pieces, columns, probes), bf16),
            pltpu.VMEM((columns, rows), f32),
            pltpu.SemaphoreType.DMA((pieces + 1,)),
        ],
        0,
        MB // 4,
        58 * MB,
    )(in_hbm(residual), in_hbm(noise_weights.T))
    h1, h3, h2 = [eastward(weighted, by) for by in (1, 3, 2)]
    flops = 2 * probes * cells * every
    acc = call(
        first_body,
        shape((probes, every), f32),
        [VMEM, HBM],
        [pltpu.VMEM((cells, every), bf16), pltpu.SemaphoreType.DMA((4,))],
        flops,
        3 * MB,
        8 * MB,
    )(weighted, in_hbm(kernel))
    flops = 6 * probes * cells * cells
    far = call(far_body, shape((probes, cells), bf16), [VMEM] * 5, [], flops, 2 * MB, 8 * MB)(
        h2, h3, h1, kernel, acc
    )
    other_far = swapped(far, 1)
    near, mine = call(
        rest_body,
        (shape((probes, cells), bf16), shape((2, probes, cells), f32)),
        [VMEM] * 5,
        [],
        3 * flops,
        6 * MB,
        8 * MB,
    )(h2, h3, h1, kernel, acc)
    packed = call(pack_body, shape((probes, cells), bf16), [VMEM] * 2, [], 0, MB, 4 * MB)(mine, other_far)
    third = swapped(packed, 2)
    other_near = swapped(near, 1)
    total = call(final_body, shape((cells, probes), f32), [VMEM] * 3, [], 0, MB, 4 * MB)(
        mine, other_near, third
    )
    return total.reshape(1, rows, columns, probes)


def solution(mesh):
    return jax.shard_map(
        per_device,
        mesh=mesh,
        in_specs=(P("lat", "lon", None), P("lat", "lon"), P(None, None, "lat", None)),
        out_specs=P(None, "lat", "lon", None),
        check_vma=False,
    )
```

```python
import jax
import jax.numpy as jnp
from jax import lax
from jax.experimental import pallas as pl
from jax.experimental.pallas import tpu as pltpu
from jax.sharding import PartitionSpec as P


VMEM = pl.BlockSpec(memory_space=pltpu.VMEM)
HBM = pl.BlockSpec(memory_space=pltpu.HBM)


def in_hbm(value):
    return pltpu.with_memory_space_constraint(value, pltpu.HBM)


def eastward(value, by):
    length = lax.axis_size("lon")
    return lax.ppermute(value, "lon", [(i, (i + by) % length) for i in range(length)])


def swapped(value, mask):
    length = lax.axis_size("lat")
    return lax.ppermute(value, "lat", [(i, i ^ mask) for i in range(length)])


def eastward_swapped(value, by, mask):
    lats, lons = lax.axis_size("lat"), lax.axis_size("lon")
    pairs = [
        (b * lons + j, (b ^ mask) * lons + (j + by) % lons) for b in range(lats) for j in range(lons)
    ]
    return lax.ppermute(value, ("lat", "lon"), pairs)


def call(body, outs, in_specs, scratch, flops, nbytes, limit):
    return pl.pallas_call(
        body,
        out_shape=outs,
        in_specs=in_specs,
        out_specs=jax.tree.map(lambda _: VMEM, outs),
        scratch_shapes=scratch,
        cost_estimate=pl.CostEstimate(flops=flops, bytes_accessed=nbytes, transcendentals=0),
        compiler_params=pltpu.CompilerParams(vmem_limit_bytes=limit),
    )


def weighted_part(data, weights, first):
    part = [
        (weights[:, first + y : first + y + 1] * data[y].astype(jnp.float32)).astype(jnp.bfloat16)
        for y in range(data.shape[0])
    ]
    return jnp.concatenate(part, axis=0).T


def product(weighted, panel):
    return jnp.dot(weighted, panel, preferred_element_type=jnp.float32)


def bands(cells):
    band = lax.axis_index("lat")
    partner = band + 1 - 2 * (band % 2)
    order = (band, 3 - partner, partner, 3 - band)
    return [pl.ds(pl.multiple_of(b * cells, cells), cells) for b in order]


def early_body(residual, noise, panels, here, east, staged, data, weights, held, weighted, sems):
    pieces, rows = data.shape[0], data.shape[1]
    cells = rows * data.shape[2]
    copies = [pltpu.make_async_copy(noise, weights, sems.at[0])]
    for i in range(pieces):
        source = residual.at[pl.ds(i * rows, rows)]
        copies.append(pltpu.make_async_copy(source, data.at[i], sems.at[1 + i]))
    for d in range(4):
        target = held.at[d] if d < 2 else staged.at[d - 2]
        copies.append(pltpu.make_async_copy(panels.at[d, 0], target, sems.at[1 + pieces + d]))
    for copy in copies:
        copy.start()
    copies[0].wait()
    for i in range(pieces):
        copies[1 + i].wait()
        weighted[:, i * cells : (i + 1) * cells] = weighted_part(data.at[i], weights, i * rows)
    block = weighted.shape[1]
    for d, acc in ((0, here), (1, east)):
        copies[1 + pieces + d].wait()
        for k in range(panels.shape[3] // block):
            where = slice(k * block, (k + 1) * block)
            acc[:, where] = product(weighted[...], held[d, :, where])
    for d in (2, 3):
        copies[1 + pieces + d].wait()


def partner_east_body(data, weights, staged, east, weighted, out):
    weighted[...] = weighted_part(data, weights, 0)
    _, _, near, far = bands(weighted.shape[1])
    for i, where in enumerate((near, far)):
        total = east[:, where] + product(weighted[...], staged[1, :, where])
        out[i] = total.astype(out.dtype)


def rest_body(weighted, staged, here, east, away, mine):
    own, own_far, near, far = bands(weighted.shape[1])
    for i, where in enumerate((far, near)):
        total = here[:, where] + product(weighted[...], staged[0, :, where])
        away[i] = total.astype(away.dtype)
    for i, where in enumerate((own, own_far)):
        mine[i] = east[:, where] + product(weighted[...], staged[1, :, where])
    for i, where in enumerate((own, own_far)):
        mine[2 + i] = here[:, where] + product(weighted[...], staged[0, :, where])


def pack_east_body(mine, other, near, far):
    near[...] = (mine[0] + other[0].astype(jnp.float32)).astype(near.dtype)
    far[...] = (mine[1] + other[1].astype(jnp.float32)).astype(far.dtype)


def pack_here_body(mine, other, far):
    far[...] = (mine[3] + other[0].astype(jnp.float32)).astype(far.dtype)


def final_body(mine, other, r1, r2, r3, out):
    total = mine[2] + other[1].astype(jnp.float32)
    for r in (r1, r2, r3):
        total += r[...].astype(jnp.float32)
    out[...] = total.T


def sweep(residual, noise_weights, kernel):
    rows, columns, probes = residual.shape
    cells = rows * columns
    every = kernel.shape[3]
    f32, bf16 = jnp.float32, jnp.bfloat16
    shape = jax.ShapeDtypeStruct
    MB = 1 << 20
    pieces = 4
    noise = noise_weights.T

    data2 = eastward(residual, 2)
    noise2 = eastward(noise, 2)
    part = shape((probes, cells), bf16)
    flops = 2 * probes * cells * cells
    here, east, staged = call(
        early_body,
        (shape((probes, every), f32), shape((probes, every), f32), shape((2, cells, every), bf16)),
        [HBM] * 3,
        [
            pltpu.VMEM((pieces, rows // pieces, columns, probes), bf16),
            pltpu.VMEM((columns, rows), f32),
            pltpu.VMEM((2, cells, every), bf16),
            pltpu.VMEM((probes, cells), bf16),
            pltpu.SemaphoreType.DMA((pieces + 5,)),
        ],
        8 * flops,
        10 * MB,
        16 * MB,
    )(in_hbm(residual), in_hbm(noise), in_hbm(kernel))
    weighted2, away = call(
        partner_east_body, (part, shape((2, probes, cells), bf16)), [VMEM] * 4, [], 2 * flops, 2 * MB, 8 * MB
    )(data2, noise2, staged, east)
    other_east = swapped(away, 1)
    away, mine = call(
        rest_body,
        (shape((2, probes, cells), bf16), shape((4, probes, cells), f32)),
        [VMEM] * 4,
        [],
        6 * flops,
        6 * MB,
        8 * MB,
    )(weighted2, staged, here, east)
    other_here = swapped(away, 1)
    near, far = call(pack_east_body, (part, part), [VMEM] * 2, [], 0, MB, 4 * MB)(mine, other_east)
    r1 = eastward(near, 1)
    r2 = eastward_swapped(far, 1, 2)
    far = call(pack_here_body, part, [VMEM] * 2, [], 0, MB, 4 * MB)(mine, other_here)
    r3 = swapped(far, 2)
    total = call(final_body, shape((cells, probes), f32), [VMEM] * 5, [], 0, MB, 4 * MB)(
        mine, other_here, r3, r2, r1
    )
    return total.reshape(1, rows, columns, probes)


def solution(mesh):
    return jax.shard_map(
        sweep,
        mesh=mesh,
        in_specs=(P("lat", "lon", None), P("lat", "lon"), P(None, None, "lat", None)),
        out_specs=P(None, "lat", "lon", None),
        check_vma=False,
    )
```

```python
import jax
import jax.numpy as jnp
from jax import lax
from jax.experimental import pallas as pl
from jax.experimental.pallas import tpu as pltpu
from jax.sharding import PartitionSpec as P


VMEM = pl.BlockSpec(memory_space=pltpu.VMEM)
HBM = pl.BlockSpec(memory_space=pltpu.HBM)


def in_hbm(value):
    return pltpu.with_memory_space_constraint(value, pltpu.HBM)


def eastward(value, by):
    length = lax.axis_size("lon")
    return lax.ppermute(value, "lon", [(i, (i + by) % length) for i in range(length)])


def swapped(value, mask):
    length = lax.axis_size("lat")
    return lax.ppermute(value, "lat", [(i, i ^ mask) for i in range(length)])


def call(body, outs, in_specs, scratch, flops, nbytes, limit):
    return pl.pallas_call(
        body,
        out_shape=outs,
        in_specs=in_specs,
        out_specs=jax.tree.map(lambda _: VMEM, outs),
        scratch_shapes=scratch,
        cost_estimate=pl.CostEstimate(flops=flops, bytes_accessed=nbytes, transcendentals=0),
        compiler_params=pltpu.CompilerParams(vmem_limit_bytes=limit),
    )


def weigh_body(residual, noise, out, data, weights, sems):
    pieces, rows = data.shape[0], data.shape[1]
    first = pltpu.make_async_copy(noise, weights, sems.at[pieces])
    first.start()
    copies = [
        pltpu.make_async_copy(residual.at[pl.ds(i * rows, rows)], data.at[i], sems.at[i])
        for i in range(pieces)
    ]
    for copy in copies:
        copy.start()
    first.wait()
    cells = rows * data.shape[2]
    for i, copy in enumerate(copies):
        copy.wait()
        part = [
            weights[:, i * rows + y : i * rows + y + 1] * data[i, y].astype(jnp.float32)
            for y in range(rows)
        ]
        out[:, i * cells : (i + 1) * cells] = jnp.concatenate(part, axis=0).T.astype(out.dtype)


def first_body(weighted, panels, acc, own, sems):
    cells = weighted.shape[1]
    depth = cells // sems.shape[0]
    copies = [
        pltpu.make_async_copy(
            panels.at[0, 0, pl.ds(i * depth, depth)], own.at[pl.ds(i * depth, depth)], sems.at[i]
        )
        for i in range(sems.shape[0])
    ]
    for copy in copies:
        copy.start()
    for copy in copies:
        copy.wait()
    for k in range(panels.shape[3] // cells):
        where = slice(k * cells, (k + 1) * cells)
        acc[:, where] = jnp.dot(weighted[...], own[:, where], preferred_element_type=jnp.float32)


def band_sum(halo, panels, acc, band, cells):
    where = pl.ds(pl.multiple_of(band * cells, cells), cells)
    total = acc[:, where]
    for d, h in enumerate(halo):
        total += jnp.dot(h[...], panels[d + 1, 0, :, where], preferred_element_type=jnp.float32)
    return total


def far_body(h2, h1, h3, panels, acc, out):
    band = 3 - lax.axis_index("lat")
    out[...] = band_sum((h1, h2, h3), panels, acc, band, h1.shape[1]).astype(out.dtype)


def rest_body(h2, h1, h3, panels, acc, near, mine):
    band = lax.axis_index("lat")
    partner = band + 1 - 2 * (band % 2)
    halo, cells = (h1, h2, h3), h1.shape[1]
    near[...] = band_sum(halo, panels, acc, partner, cells).astype(near.dtype)
    mine[0] = band_sum(halo, panels, acc, 3 - partner, cells)
    mine[1] = band_sum(halo, panels, acc, band, cells)


def pack_body(mine, other, out):
    out[...] = (mine[0] + other[...].astype(jnp.float32)).astype(out.dtype)


def final_body(mine, other, third, out):
    total = mine[1] + other[...].astype(jnp.float32) + third[...].astype(jnp.float32)
    out[...] = total.T


def per_device(residual, noise_weights, kernel):
    rows, columns, probes = residual.shape
    cells = rows * columns
    every = kernel.shape[3]
    f32, bf16 = jnp.float32, jnp.bfloat16
    shape = jax.ShapeDtypeStruct
    MB = 1 << 20

    pieces = 4
    weighted = call(
        weigh_body,
        pltpu.VMEM((probes, cells), bf16),
        [HBM, HBM],
        [
            pltpu.VMEM((pieces, rows // pieces, columns, probes), bf16),
            pltpu.VMEM((columns, rows), f32),
            pltpu.SemaphoreType.DMA((pieces + 1,)),
        ],
        0,
        MB // 4,
        58 * MB,
    )(in_hbm(residual), in_hbm(noise_weights.T))
    h3, h1, h2 = [eastward(weighted, by) for by in (3, 1, 2)]
    flops = 2 * probes * cells * every
    acc = call(
        first_body,
        shape((probes, every), f32),
        [VMEM, HBM],
        [pltpu.VMEM((cells, every), bf16), pltpu.SemaphoreType.DMA((4,))],
        flops,
        3 * MB,
        8 * MB,
    )(weighted, in_hbm(kernel))
    flops = 6 * probes * cells * cells
    far = call(far_body, shape((probes, cells), bf16), [VMEM] * 5, [], flops, 2 * MB, 8 * MB)(
        h2, h1, h3, kernel, acc
    )
    other_far = swapped(far, 1)
    near, mine = call(
        rest_body,
        (shape((probes, cells), bf16), shape((2, probes, cells), f32)),
        [VMEM] * 5,
        [],
        3 * flops,
        6 * MB,
        8 * MB,
    )(h2, h1, h3, kernel, acc)
    packed = call(pack_body, shape((probes, cells), bf16), [VMEM] * 2, [], 0, MB, 4 * MB)(mine, other_far)
    third = swapped(packed, 2)
    other_near = swapped(near, 1)
    total = call(final_body, shape((cells, probes), f32), [VMEM] * 3, [], 0, MB, 4 * MB)(
        mine, other_near, third
    )
    return total.reshape(1, rows, columns, probes)


def solution(mesh):
    return jax.shard_map(
        per_device,
        mesh=mesh,
        in_specs=(P("lat", "lon", None), P("lat", "lon"), P(None, None, "lat", None)),
        out_specs=P(None, "lat", "lon", None),
        check_vma=False,
    )
```

```python
import jax
import jax.numpy as jnp
from jax import lax
from jax.experimental import pallas as pl
from jax.experimental.pallas import tpu as pltpu
from jax.sharding import PartitionSpec as P


SEGMENT = 8

VMEM = pl.BlockSpec(memory_space=pltpu.VMEM)
HBM = pl.BlockSpec(memory_space=pltpu.HBM)


def in_hbm(value):
    return pltpu.with_memory_space_constraint(value, pltpu.HBM)


def lon_pairs(by, wanted):
    length = lax.axis_size("lon")
    return [((i - by) % length, i) for i in range(length) if wanted(i % SEGMENT == 0)]


def eastward(value, by, wanted=lambda first: True):
    return lax.ppermute(value, "lon", lon_pairs(by, wanted))


def swapped(value, mask):
    length = lax.axis_size("lat")
    return lax.ppermute(value, "lat", [(i, i ^ mask) for i in range(length)])


def eastward_swapped(value, by, mask, wanted):
    lats, lons = lax.axis_size("lat"), lax.axis_size("lon")
    pairs = [(b * lons + i, (b ^ mask) * lons + j) for b in range(lats) for i, j in lon_pairs(by, wanted)]
    return lax.ppermute(value, ("lat", "lon"), pairs)


def call(body, outs, in_specs, scratch, flops, nbytes, limit):
    return pl.pallas_call(
        body,
        out_shape=outs,
        in_specs=in_specs,
        out_specs=jax.tree.map(lambda _: VMEM, outs),
        scratch_shapes=scratch,
        cost_estimate=pl.CostEstimate(flops=flops, bytes_accessed=nbytes, transcendentals=0),
        compiler_params=pltpu.CompilerParams(vmem_limit_bytes=limit),
    )


def weigh_body(residual, noise, out, data, weights, sems):
    copies = [
        pltpu.make_async_copy(noise, weights, sems.at[0]),
        pltpu.make_async_copy(residual, data, sems.at[1]),
    ]
    for copy in copies:
        copy.start()
    for copy in copies:
        copy.wait()
    part = [
        (weights[:, y : y + 1] * data[y].astype(jnp.float32)).astype(out.dtype)
        for y in range(data.shape[0])
    ]
    out[...] = jnp.concatenate(part, axis=0).T


def product(weighted, panel):
    return jnp.dot(weighted, panel, preferred_element_type=jnp.float32)


def bands(cells):
    band = lax.axis_index("lat")
    partner = band + 1 - 2 * (band % 2)
    order = (band, 3 - partner, partner, 3 - band)
    return [pl.ds(pl.multiple_of(b * cells, cells), cells) for b in order]


def early_body(weighted, panels, here, east, staged, held, sems):
    copies = [pltpu.make_async_copy(panels.at[0, 0], held, sems.at[0])]
    for d in range(1, 4):
        copies.append(pltpu.make_async_copy(panels.at[d, 0], staged.at[d - 1], sems.at[d]))
    for copy in copies:
        copy.start()
    block = weighted.shape[1]
    for d, acc, panel in ((0, here, held), (1, east, staged.at[0])):
        copies[d].wait()
        for k in range(panels.shape[3] // block):
            where = slice(k * block, (k + 1) * block)
            acc[:, where] = product(weighted[...], panel[:, where])
    for copy in copies[2:]:
        copy.wait()


def partner_east_body(weighted, staged, east, out):
    _, _, near, far = bands(weighted.shape[1])
    for i, where in enumerate((near, far)):
        total = east[:, where] + product(weighted[...], staged[2, :, where])
        out[i] = total.astype(out.dtype)


def rest_body(weighted, w1, w3, staged, here, east, away, mine, total):
    own, own_far, near, far = bands(weighted.shape[1])
    for i, where in enumerate((own, own_far)):
        mine[i] = east[:, where] + product(weighted[...], staged[2, :, where])
    order = (own, own_far, far, near)
    for i, where in enumerate(order):
        total[i] = here[:, where] + product(weighted[...], staged[1, :, where])

    @pl.when(lax.axis_index("lon") % SEGMENT == 0)
    def _():
        for i, where in enumerate(order):
            total[i] += product(w1[...], staged[0, :, where]) + product(w3[...], staged[2, :, where])

    for i in range(2):
        mine[2 + i] = total[i]
        away[i] = total[2 + i].astype(away.dtype)


def pack_east_body(mine, other, near, far):
    near[...] = (mine[0] + other[0].astype(jnp.float32)).astype(near.dtype)
    far[...] = (mine[1] + other[1].astype(jnp.float32)).astype(far.dtype)


def pack_here_body(mine, other, far):
    far[...] = (mine[3] + other[0].astype(jnp.float32)).astype(far.dtype)


def final_body(mine, other, r1, r2, r3, out):
    total = mine[2] + other[1].astype(jnp.float32)
    for r in (r1, r2, r3):
        total += r[...].astype(jnp.float32)
    out[...] = total.T


def sweep(residual, noise_weights, kernel):
    rows, columns, probes = residual.shape
    cells = rows * columns
    every = kernel.shape[3]
    f32, bf16 = jnp.float32, jnp.bfloat16
    shape = jax.ShapeDtypeStruct
    MB = 1 << 20
    part = shape((probes, cells), bf16)
    flops = 2 * probes * cells * cells

    weighted = call(
        weigh_body,
        pltpu.VMEM((probes, cells), bf16),
        [HBM] * 2,
        [
            pltpu.VMEM((rows, columns, probes), bf16),
            pltpu.VMEM((columns, rows), f32),
            pltpu.SemaphoreType.DMA((2,)),
        ],
        0,
        MB // 4,
        4 * MB,
    )(in_hbm(residual), in_hbm(noise_weights.T))
    w2 = eastward(weighted, 2)
    w1 = eastward(weighted, 1, lambda first: first)
    w3 = eastward(weighted, 3, lambda first: first)
    here, east, staged = call(
        early_body,
        (shape((probes, every), f32), shape((probes, every), f32), shape((3, cells, every), bf16)),
        [VMEM, HBM],
        [pltpu.VMEM((cells, every), bf16), pltpu.SemaphoreType.DMA((4,))],
        8 * flops,
        10 * MB,
        16 * MB,
    )(weighted, in_hbm(kernel))
    away = call(partner_east_body, shape((2, probes, cells), bf16), [VMEM] * 3, [], 2 * flops, 2 * MB, 8 * MB)(
        w2, staged, east
    )
    other_east = swapped(away, 1)
    away, mine = call(
        rest_body,
        (shape((2, probes, cells), bf16), shape((4, probes, cells), f32)),
        [VMEM] * 6,
        [pltpu.VMEM((4, probes, cells), f32)],
        6 * flops,
        6 * MB,
        8 * MB,
    )(w2, w1, w3, staged, here, east)
    other_here = swapped(away, 1)
    near, far = call(pack_east_body, (part, part), [VMEM] * 2, [], 0, MB, 4 * MB)(mine, other_east)
    r1 = eastward(near, 1, lambda first: not first)
    r2 = eastward_swapped(far, 1, 2, lambda first: not first)
    far = call(pack_here_body, part, [VMEM] * 2, [], 0, MB, 4 * MB)(mine, other_here)
    r3 = swapped(far, 2)
    total = call(final_body, shape((cells, probes), f32), [VMEM] * 5, [], 0, MB, 4 * MB)(
        mine, other_here, r3, r2, r1
    )
    return total.reshape(1, rows, columns, probes)


def solution(mesh):
    return jax.shard_map(
        sweep,
        mesh=mesh,
        in_specs=(P("lat", "lon", None), P("lat", "lon"), P(None, None, "lat", None)),
        out_specs=P(None, "lat", "lon", None),
        check_vma=False,
    )
```

```python
import jax
import jax.numpy as jnp
from jax import lax
from jax.experimental import pallas as pl
from jax.experimental.pallas import tpu as pltpu
from jax.sharding import PartitionSpec as P


VMEM = pl.BlockSpec(memory_space=pltpu.VMEM)
HBM = pl.BlockSpec(memory_space=pltpu.HBM)


def in_hbm(value):
    return pltpu.with_memory_space_constraint(value, pltpu.HBM)


def eastward(value, by):
    length = lax.axis_size("lon")
    return lax.ppermute(value, "lon", [(i, (i + by) % length) for i in range(length)])


def swapped(value, mask):
    length = lax.axis_size("lat")
    return lax.ppermute(value, "lat", [(i, i ^ mask) for i in range(length)])


def call(body, outs, in_specs, scratch, flops, nbytes, limit):
    return pl.pallas_call(
        body,
        out_shape=outs,
        in_specs=in_specs,
        out_specs=jax.tree.map(lambda _: VMEM, outs),
        scratch_shapes=scratch,
        cost_estimate=pl.CostEstimate(flops=flops, bytes_accessed=nbytes, transcendentals=0),
        compiler_params=pltpu.CompilerParams(vmem_limit_bytes=limit),
    )


def weigh_body(residual, noise, out, data, weights, sems):
    copies = [
        pltpu.make_async_copy(noise, weights, sems.at[0]),
        pltpu.make_async_copy(residual, data, sems.at[1]),
    ]
    for copy in copies:
        copy.start()
    for copy in copies:
        copy.wait()
    part = [
        (weights[:, y : y + 1] * data[y].astype(jnp.float32)).astype(out.dtype)
        for y in range(data.shape[0])
    ]
    out[...] = jnp.concatenate(part, axis=0).T


def first_body(weighted, panels, acc, own, sems):
    cells = weighted.shape[1]
    depth = cells // sems.shape[0]
    copies = [
        pltpu.make_async_copy(
            panels.at[0, 0, pl.ds(i * depth, depth)], own.at[pl.ds(i * depth, depth)], sems.at[i]
        )
        for i in range(sems.shape[0])
    ]
    for copy in copies:
        copy.start()
    for copy in copies:
        copy.wait()
    for k in range(panels.shape[3] // cells):
        where = slice(k * cells, (k + 1) * cells)
        acc[:, where] = jnp.dot(weighted[...], own[:, where], preferred_element_type=jnp.float32)


def band_sum(halo, panels, acc, band, cells):
    where = pl.ds(pl.multiple_of(band * cells, cells), cells)
    total = acc[:, where]
    for d, h in enumerate(halo):
        total += jnp.dot(h[...], panels[d + 1, 0, :, where], preferred_element_type=jnp.float32)
    return total


def far_body(h2, h3, h1, panels, acc, out):
    band = 3 - lax.axis_index("lat")
    out[...] = band_sum((h1, h2, h3), panels, acc, band, h1.shape[1]).astype(out.dtype)


def rest_body(h2, h3, h1, panels, acc, near, mine):
    band = lax.axis_index("lat")
    partner = band + 1 - 2 * (band % 2)
    halo, cells = (h1, h2, h3), h1.shape[1]
    near[...] = band_sum(halo, panels, acc, partner, cells).astype(near.dtype)
    mine[0] = band_sum(halo, panels, acc, 3 - partner, cells)
    mine[1] = band_sum(halo, panels, acc, band, cells)


def pack_body(mine, other, out):
    out[...] = (mine[0] + other[...].astype(jnp.float32)).astype(out.dtype)


def final_body(mine, other, third, out):
    total = mine[1] + other[...].astype(jnp.float32) + third[...].astype(jnp.float32)
    out[...] = total.T


def sweep(residual, noise_weights, kernel):
    rows, columns, probes = residual.shape
    cells = rows * columns
    every = kernel.shape[3]
    f32, bf16 = jnp.float32, jnp.bfloat16
    shape = jax.ShapeDtypeStruct
    MB = 1 << 20

    weighted = call(
        weigh_body,
        pltpu.VMEM((probes, cells), bf16),
        [HBM] * 2,
        [
            pltpu.VMEM((rows, columns, probes), bf16),
            pltpu.VMEM((columns, rows), f32),
            pltpu.SemaphoreType.DMA((2,)),
        ],
        0,
        MB // 4,
        58 * MB,
    )(in_hbm(residual), in_hbm(noise_weights.T))
    h1, h3, h2 = [eastward(weighted, by) for by in (1, 3, 2)]
    flops = 2 * probes * cells * every
    acc = call(
        first_body,
        shape((probes, every), f32),
        [VMEM, HBM],
        [pltpu.VMEM((cells, every), bf16), pltpu.SemaphoreType.DMA((4,))],
        flops,
        3 * MB,
        8 * MB,
    )(weighted, in_hbm(kernel))
    flops = 6 * probes * cells * cells
    far = call(far_body, shape((probes, cells), bf16), [VMEM] * 5, [], flops, 2 * MB, 8 * MB)(
        h2, h3, h1, kernel, acc
    )
    other_far = swapped(far, 1)
    near, mine = call(
        rest_body,
        (shape((probes, cells), bf16), shape((2, probes, cells), f32)),
        [VMEM] * 5,
        [],
        3 * flops,
        6 * MB,
        8 * MB,
    )(h2, h3, h1, kernel, acc)
    packed = call(pack_body, shape((probes, cells), bf16), [VMEM] * 2, [], 0, MB, 4 * MB)(mine, other_far)
    third = swapped(packed, 2)
    other_near = swapped(near, 1)
    total = call(final_body, shape((cells, probes), f32), [VMEM] * 3, [], 0, MB, 4 * MB)(
        mine, other_near, third
    )
    return total.reshape(1, rows, columns, probes)


def solution(mesh):
    return jax.shard_map(
        sweep,
        mesh=mesh,
        in_specs=(P("lat", "lon", None), P("lat", "lon"), P(None, None, "lat", None)),
        out_specs=P(None, "lat", "lon", None),
        check_vma=False,
    )
```

```python
import jax
import jax.numpy as jnp
from jax import lax
from jax.experimental import pallas as pl
from jax.experimental.pallas import tpu as pltpu
from jax.sharding import PartitionSpec as P


VMEM = pl.BlockSpec(memory_space=pltpu.VMEM)
HBM = pl.BlockSpec(memory_space=pltpu.HBM)


def in_hbm(value):
    return pltpu.with_memory_space_constraint(value, pltpu.HBM)


def eastward(value, even, odd):
    length = lax.axis_size("lon")
    pairs = [(i, (i + (odd if i % 2 else even)) % length) for i in range(length)]
    return lax.ppermute(value, "lon", pairs)


def swapped(value, mask):
    length = lax.axis_size("lat")
    return lax.ppermute(value, "lat", [(i, i ^ mask) for i in range(length)])


def call(body, outs, in_specs, scratch, flops, nbytes, limit):
    return pl.pallas_call(
        body,
        out_shape=outs,
        in_specs=in_specs,
        out_specs=jax.tree.map(lambda _: VMEM, outs),
        scratch_shapes=scratch,
        cost_estimate=pl.CostEstimate(flops=flops, bytes_accessed=nbytes, transcendentals=0),
        compiler_params=pltpu.CompilerParams(vmem_limit_bytes=limit),
    )


def weigh_body(residual, noise, out, data, weights, sems):
    copies = [
        pltpu.make_async_copy(noise, weights, sems.at[0]),
        pltpu.make_async_copy(residual, data, sems.at[1]),
    ]
    for copy in copies:
        copy.start()
    for copy in copies:
        copy.wait()
    part = [
        (weights[:, y : y + 1] * data[y].astype(jnp.float32)).astype(out.dtype)
        for y in range(data.shape[0])
    ]
    out[...] = jnp.concatenate(part, axis=0).T


def first_body(weighted, panels, acc, own, sems):
    cells = weighted.shape[1]
    depth = cells // sems.shape[0]
    copies = [
        pltpu.make_async_copy(
            panels.at[0, 0, pl.ds(i * depth, depth)], own.at[pl.ds(i * depth, depth)], sems.at[i]
        )
        for i in range(sems.shape[0])
    ]
    for copy in copies:
        copy.start()
    for copy in copies:
        copy.wait()
    for k in range(panels.shape[3] // cells):
        where = slice(k * cells, (k + 1) * cells)
        acc[:, where] = jnp.dot(weighted[...], own[:, where], preferred_element_type=jnp.float32)


def band_sum(halo, panels, acc, band, cells):
    where = pl.ds(pl.multiple_of(band * cells, cells), cells)
    odd = lax.axis_index("lon") % 2
    total = acc[:, where]
    for d, h in zip((3 - 2 * odd, 1 + 2 * odd, 2), halo):
        total += jnp.dot(h[...], panels[d, 0, :, where], preferred_element_type=jnp.float32)
    return total


def far_body(h2, hb, ha, panels, acc, out):
    band = 3 - lax.axis_index("lat")
    out[...] = band_sum((ha, hb, h2), panels, acc, band, h2.shape[1]).astype(out.dtype)


def rest_body(h2, hb, ha, panels, acc, near, mine):
    band = lax.axis_index("lat")
    partner = band + 1 - 2 * (band % 2)
    halo, cells = (ha, hb, h2), h2.shape[1]
    near[...] = band_sum(halo, panels, acc, partner, cells).astype(near.dtype)
    mine[0] = band_sum(halo, panels, acc, 3 - partner, cells)
    mine[1] = band_sum(halo, panels, acc, band, cells)


def pack_body(mine, other, out):
    out[...] = (mine[0] + other[...].astype(jnp.float32)).astype(out.dtype)


def final_body(mine, other, third, out):
    total = mine[1] + other[...].astype(jnp.float32) + third[...].astype(jnp.float32)
    out[...] = total.T


def sweep(residual, noise_weights, kernel):
    rows, columns, probes = residual.shape
    cells = rows * columns
    every = kernel.shape[3]
    f32, bf16 = jnp.float32, jnp.bfloat16
    shape = jax.ShapeDtypeStruct
    MB = 1 << 20

    weighted = call(
        weigh_body,
        pltpu.VMEM((probes, cells), bf16),
        [HBM] * 2,
        [
            pltpu.VMEM((rows, columns, probes), bf16),
            pltpu.VMEM((columns, rows), f32),
            pltpu.SemaphoreType.DMA((2,)),
        ],
        0,
        MB // 4,
        58 * MB,
    )(in_hbm(residual), in_hbm(noise_weights.T))
    ha = eastward(weighted, 1, 3)
    hb = eastward(weighted, 3, 1)
    h2 = eastward(weighted, 2, 2)
    flops = 2 * probes * cells * every
    acc = call(
        first_body,
        shape((probes, every), f32),
        [VMEM, HBM],
        [pltpu.VMEM((cells, every), bf16), pltpu.SemaphoreType.DMA((4,))],
        flops,
        3 * MB,
        8 * MB,
    )(weighted, in_hbm(kernel))
    flops = 6 * probes * cells * cells
    far = call(far_body, shape((probes, cells), bf16), [VMEM] * 5, [], flops, 2 * MB, 8 * MB)(
        h2, hb, ha, kernel, acc
    )
    other_far = swapped(far, 1)
    near, mine = call(
        rest_body,
        (shape((probes, cells), bf16), shape((2, probes, cells), f32)),
        [VMEM] * 5,
        [],
        3 * flops,
        6 * MB,
        8 * MB,
    )(h2, hb, ha, kernel, acc)
    packed = call(pack_body, shape((probes, cells), bf16), [VMEM] * 2, [], 0, MB, 4 * MB)(mine, other_far)
    third = swapped(packed, 2)
    other_near = swapped(near, 1)
    total = call(final_body, shape((cells, probes), f32), [VMEM] * 3, [], 0, MB, 4 * MB)(
        mine, other_near, third
    )
    return total.reshape(1, rows, columns, probes)


def solution(mesh):
    return jax.shard_map(
        sweep,
        mesh=mesh,
        in_specs=(P("lat", "lon", None), P("lat", "lon"), P(None, None, "lat", None)),
        out_specs=P(None, "lat", "lon", None),
        check_vma=False,
    )
```

```python
import jax
import jax.numpy as jnp
from jax import lax
from jax.experimental import pallas as pl
from jax.experimental.pallas import tpu as pltpu
from jax.sharding import PartitionSpec as P


SHIFTS = ((3, 1), (1, 3), (2, 2))

VMEM = pl.BlockSpec(memory_space=pltpu.VMEM)
HBM = pl.BlockSpec(memory_space=pltpu.HBM)


def in_hbm(value):
    return pltpu.with_memory_space_constraint(value, pltpu.HBM)


def eastward(value, even, odd):
    length = lax.axis_size("lon")
    pairs = [(i, (i + (odd if i % 2 else even)) % length) for i in range(length)]
    return lax.ppermute(value, "lon", pairs)


def swapped(value, mask):
    length = lax.axis_size("lat")
    return lax.ppermute(value, "lat", [(i, i ^ mask) for i in range(length)])


def call(body, outs, in_specs, scratch, flops, nbytes, limit):
    return pl.pallas_call(
        body,
        out_shape=outs,
        in_specs=in_specs,
        out_specs=jax.tree.map(lambda _: VMEM, outs),
        scratch_shapes=scratch,
        cost_estimate=pl.CostEstimate(flops=flops, bytes_accessed=nbytes, transcendentals=0),
        compiler_params=pltpu.CompilerParams(vmem_limit_bytes=limit),
    )


def weigh_body(residual, noise, out, data, weights, sems):
    copies = [
        pltpu.make_async_copy(noise, weights, sems.at[0]),
        pltpu.make_async_copy(residual, data, sems.at[1]),
    ]
    for copy in copies:
        copy.start()
    for copy in copies:
        copy.wait()
    part = [
        (weights[:, y : y + 1] * data[y].astype(jnp.float32)).astype(out.dtype)
        for y in range(data.shape[0])
    ]
    out[...] = jnp.concatenate(part, axis=0).T


def first_body(weighted, panels, acc, own, sems):
    cells = weighted.shape[1]
    depth = cells // sems.shape[0]
    copies = [
        pltpu.make_async_copy(
            panels.at[0, 0, pl.ds(i * depth, depth)], own.at[pl.ds(i * depth, depth)], sems.at[i]
        )
        for i in range(sems.shape[0])
    ]
    for copy in copies:
        copy.start()
    for copy in copies:
        copy.wait()
    for k in range(panels.shape[3] // cells):
        where = slice(k * cells, (k + 1) * cells)
        acc[:, where] = jnp.dot(weighted[...], own[:, where], preferred_element_type=jnp.float32)


def band_sum(halo, panels, acc, band, cells):
    where = pl.ds(pl.multiple_of(band * cells, cells), cells)
    odd = lax.axis_index("lon") % 2
    total = acc[:, where]
    for (from_even, from_odd), h in zip(SHIFTS, halo):
        d = from_odd + (from_even - from_odd) * odd
        total += jnp.dot(h[...], panels[d, 0, :, where], preferred_element_type=jnp.float32)
    return total


def far_body(ha, hb, hc, panels, acc, out):
    band = 3 - lax.axis_index("lat")
    out[...] = band_sum((ha, hb, hc), panels, acc, band, ha.shape[1]).astype(out.dtype)


def rest_body(ha, hb, hc, panels, acc, near, mine):
    band = lax.axis_index("lat")
    partner = band + 1 - 2 * (band % 2)
    halo, cells = (ha, hb, hc), ha.shape[1]
    near[...] = band_sum(halo, panels, acc, partner, cells).astype(near.dtype)
    mine[0] = band_sum(halo, panels, acc, 3 - partner, cells)
    mine[1] = band_sum(halo, panels, acc, band, cells)


def pack_body(mine, other, out):
    out[...] = (mine[0] + other[...].astype(jnp.float32)).astype(out.dtype)


def final_body(mine, other, third, out):
    total = mine[1] + other[...].astype(jnp.float32) + third[...].astype(jnp.float32)
    out[...] = total.T


def sweep(residual, noise_weights, kernel):
    rows, columns, probes = residual.shape
    cells = rows * columns
    every = kernel.shape[3]
    f32, bf16 = jnp.float32, jnp.bfloat16
    shape = jax.ShapeDtypeStruct
    MB = 1 << 20

    weighted = call(
        weigh_body,
        pltpu.VMEM((probes, cells), bf16),
        [HBM] * 2,
        [
            pltpu.VMEM((rows, columns, probes), bf16),
            pltpu.VMEM((columns, rows), f32),
            pltpu.SemaphoreType.DMA((2,)),
        ],
        0,
        MB // 4,
        58 * MB,
    )(in_hbm(residual), in_hbm(noise_weights.T))
    halo = []
    for shifts in SHIFTS:
        halo.append(eastward(weighted, *shifts))
    ha, hb, hc = halo
    flops = 2 * probes * cells * every
    acc = call(
        first_body,
        shape((probes, every), f32),
        [VMEM, HBM],
        [pltpu.VMEM((cells, every), bf16), pltpu.SemaphoreType.DMA((4,))],
        flops,
        3 * MB,
        8 * MB,
    )(weighted, in_hbm(kernel))
    flops = 6 * probes * cells * cells
    far = call(far_body, shape((probes, cells), bf16), [VMEM] * 5, [], flops, 2 * MB, 8 * MB)(
        ha, hb, hc, kernel, acc
    )
    other_far = swapped(far, 1)
    near, mine = call(
        rest_body,
        (shape((probes, cells), bf16), shape((2, probes, cells), f32)),
        [VMEM] * 5,
        [],
        3 * flops,
        6 * MB,
        8 * MB,
    )(ha, hb, hc, kernel, acc)
    packed = call(pack_body, shape((probes, cells), bf16), [VMEM] * 2, [], 0, MB, 4 * MB)(mine, other_far)
    third = swapped(packed, 2)
    other_near = swapped(near, 1)
    total = call(final_body, shape((cells, probes), f32), [VMEM] * 3, [], 0, MB, 4 * MB)(
        mine, other_near, third
    )
    return total.reshape(1, rows, columns, probes)


def solution(mesh):
    return jax.shard_map(
        sweep,
        mesh=mesh,
        in_specs=(P("lat", "lon", None), P("lat", "lon"), P(None, None, "lat", None)),
        out_specs=P(None, "lat", "lon", None),
        check_vma=False,
    )
```

```python
import jax
import jax.numpy as jnp
from jax import lax
from jax.experimental import pallas as pl
from jax.experimental.pallas import tpu as pltpu
from jax.sharding import PartitionSpec as P


SHIFTS = ((3, 1), (1, 3), (2, 2))

VMEM = pl.BlockSpec(memory_space=pltpu.VMEM)
HBM = pl.BlockSpec(memory_space=pltpu.HBM)


def in_hbm(value):
    return pltpu.with_memory_space_constraint(value, pltpu.HBM)


def eastward(value, even, odd):
    length = lax.axis_size("lon")
    pairs = [(i, (i + (odd if i % 2 else even)) % length) for i in range(length)]
    return lax.ppermute(value, "lon", pairs)


def swapped(value, mask):
    length = lax.axis_size("lat")
    return lax.ppermute(value, "lat", [(i, i ^ mask) for i in range(length)])


def call(body, outs, in_specs, scratch, flops, nbytes, limit):
    return pl.pallas_call(
        body,
        out_shape=outs,
        in_specs=in_specs,
        out_specs=jax.tree.map(lambda _: VMEM, outs),
        scratch_shapes=scratch,
        cost_estimate=pl.CostEstimate(flops=flops, bytes_accessed=nbytes, transcendentals=0),
        compiler_params=pltpu.CompilerParams(vmem_limit_bytes=limit),
    )


def weigh_body(residual, noise, out, data, weights, sems):
    copies = [
        pltpu.make_async_copy(noise, weights, sems.at[0]),
        pltpu.make_async_copy(residual, data, sems.at[1]),
    ]
    for copy in copies:
        copy.start()
    for copy in copies:
        copy.wait()
    part = [
        (weights[:, y : y + 1] * data[y].astype(jnp.float32)).astype(out.dtype)
        for y in range(data.shape[0])
    ]
    out[...] = jnp.concatenate(part, axis=0).T


def first_body(weighted, panels, acc, staged, own, sems):
    cells = weighted.shape[1]
    copies = [pltpu.make_async_copy(panels.at[0, 0], own, sems.at[0])]
    for d in range(1, 4):
        copies.append(pltpu.make_async_copy(panels.at[d, 0], staged.at[d - 1], sems.at[d]))
    for copy in copies:
        copy.start()
    copies[0].wait()
    for k in range(panels.shape[3] // cells):
        where = slice(k * cells, (k + 1) * cells)
        acc[:, where] = jnp.dot(weighted[...], own[:, where], preferred_element_type=jnp.float32)
    for copy in copies[1:]:
        copy.wait()


def band_sum(halo, panels, acc, band, cells):
    where = pl.ds(pl.multiple_of(band * cells, cells), cells)
    odd = lax.axis_index("lon") % 2
    total = acc[:, where]
    for (from_even, from_odd), h in zip(SHIFTS, halo):
        d = from_odd + (from_even - from_odd) * odd
        total += jnp.dot(h[...], panels[d - 1, :, where], preferred_element_type=jnp.float32)
    return total


def far_body(ha, hb, hc, panels, acc, out):
    band = 3 - lax.axis_index("lat")
    out[...] = band_sum((ha, hb, hc), panels, acc, band, ha.shape[1]).astype(out.dtype)


def rest_body(ha, hb, hc, panels, acc, near, mine):
    band = lax.axis_index("lat")
    partner = band + 1 - 2 * (band % 2)
    halo, cells = (ha, hb, hc), ha.shape[1]
    near[...] = band_sum(halo, panels, acc, partner, cells).astype(near.dtype)
    mine[0] = band_sum(halo, panels, acc, 3 - partner, cells)
    mine[1] = band_sum(halo, panels, acc, band, cells)


def pack_body(mine, other, out):
    out[...] = (mine[0] + other[...].astype(jnp.float32)).astype(out.dtype)


def final_body(mine, other, third, out):
    total = mine[1] + other[...].astype(jnp.float32) + third[...].astype(jnp.float32)
    out[...] = total.T


def sweep(residual, noise_weights, kernel):
    rows, columns, probes = residual.shape
    cells = rows * columns
    every = kernel.shape[3]
    f32, bf16 = jnp.float32, jnp.bfloat16
    shape = jax.ShapeDtypeStruct
    MB = 1 << 20

    weighted = call(
        weigh_body,
        pltpu.VMEM((probes, cells), bf16),
        [HBM] * 2,
        [
            pltpu.VMEM((rows, columns, probes), bf16),
            pltpu.VMEM((columns, rows), f32),
            pltpu.SemaphoreType.DMA((2,)),
        ],
        0,
        MB // 4,
        58 * MB,
    )(in_hbm(residual), in_hbm(noise_weights.T))
    halo = []
    for shifts in SHIFTS:
        halo.append(eastward(weighted, *shifts))
    ha, hb, hc = halo
    flops = 2 * probes * cells * every
    acc, staged = call(
        first_body,
        (shape((probes, every), f32), shape((3, cells, every), bf16)),
        [VMEM, HBM],
        [pltpu.VMEM((cells, every), bf16), pltpu.SemaphoreType.DMA((4,))],
        flops,
        9 * MB,
        16 * MB,
    )(weighted, in_hbm(kernel))
    flops = 6 * probes * cells * cells
    far = call(far_body, shape((probes, cells), bf16), [VMEM] * 5, [], flops, 2 * MB, 8 * MB)(
        ha, hb, hc, staged, acc
    )
    other_far = swapped(far, 1)
    near, mine = call(
        rest_body,
        (shape((probes, cells), bf16), shape((2, probes, cells), f32)),
        [VMEM] * 5,
        [],
        3 * flops,
        6 * MB,
        8 * MB,
    )(ha, hb, hc, staged, acc)
    packed = call(pack_body, shape((probes, cells), bf16), [VMEM] * 2, [], 0, MB, 4 * MB)(mine, other_far)
    third = swapped(packed, 2)
    other_near = swapped(near, 1)
    total = call(final_body, shape((cells, probes), f32), [VMEM] * 3, [], 0, MB, 4 * MB)(
        mine, other_near, third
    )
    return total.reshape(1, rows, columns, probes)


def solution(mesh):
    return jax.shard_map(
        sweep,
        mesh=mesh,
        in_specs=(P("lat", "lon", None), P("lat", "lon"), P(None, None, "lat", None)),
        out_specs=P(None, "lat", "lon", None),
        check_vma=False,
    )
```

```python
import functools

import jax
import jax.numpy as jnp
from jax import lax
from jax.experimental import pallas as pl
from jax.experimental.pallas import tpu as pltpu
from jax.sharding import PartitionSpec as P


SHIFTS = ((3, 1), (1, 3), (2, 2))

VMEM = pl.BlockSpec(memory_space=pltpu.VMEM)
HBM = pl.BlockSpec(memory_space=pltpu.HBM)


def in_hbm(value):
    return pltpu.with_memory_space_constraint(value, pltpu.HBM)


def eastward(value, even, odd):
    length = lax.axis_size("lon")
    pairs = [(i, (i + (odd if i % 2 else even)) % length) for i in range(length)]
    return lax.ppermute(value, "lon", pairs)


def swapped(value, mask):
    length = lax.axis_size("lat")
    return lax.ppermute(value, "lat", [(i, i ^ mask) for i in range(length)])


def call(body, outs, in_specs, scratch, flops, nbytes, limit):
    return pl.pallas_call(
        body,
        out_shape=outs,
        in_specs=in_specs,
        out_specs=jax.tree.map(lambda _: VMEM, outs),
        scratch_shapes=scratch,
        cost_estimate=pl.CostEstimate(flops=flops, bytes_accessed=nbytes, transcendentals=0),
        compiler_params=pltpu.CompilerParams(vmem_limit_bytes=limit),
    )


def weigh_body(residual, noise, out, data, weights, sems):
    copies = [
        pltpu.make_async_copy(noise, weights, sems.at[0]),
        pltpu.make_async_copy(residual, data, sems.at[1]),
    ]
    for copy in copies:
        copy.start()
    for copy in copies:
        copy.wait()
    part = [
        (weights[:, y : y + 1] * data[y].astype(jnp.float32)).astype(out.dtype)
        for y in range(data.shape[0])
    ]
    out[...] = jnp.concatenate(part, axis=0).T


def first_body(weighted, panels, acc, own, sems):
    cells = weighted.shape[1]
    depth = cells // sems.shape[0]
    copies = [
        pltpu.make_async_copy(
            panels.at[0, 0, pl.ds(i * depth, depth)], own.at[pl.ds(i * depth, depth)], sems.at[i]
        )
        for i in range(sems.shape[0])
    ]
    for copy in copies:
        copy.start()
    for copy in copies:
        copy.wait()
    for k in range(panels.shape[3] // cells):
        where = slice(k * cells, (k + 1) * cells)
        acc[:, where] = jnp.dot(weighted[...], own[:, where], preferred_element_type=jnp.float32)


def band_sum(halo, panels, acc, band, cells, part=0, parts=1):
    width = cells // parts
    where = pl.ds(pl.multiple_of(band * cells + part * width, width), width)
    odd = lax.axis_index("lon") % 2
    total = acc[:, where]
    for (from_even, from_odd), h in zip(SHIFTS, halo):
        d = from_odd + (from_even - from_odd) * odd
        total += jnp.dot(h[...], panels[d, 0, :, where], preferred_element_type=jnp.float32)
    return total


def far_body(part, ha, hb, hc, panels, acc, out):
    band = 3 - lax.axis_index("lat")
    out[...] = band_sum((ha, hb, hc), panels, acc, band, ha.shape[1], part, 2).astype(out.dtype)


def own_far_body(ha, hb, hc, panels, acc, mine):
    band = lax.axis_index("lat")
    mine[...] = band_sum((ha, hb, hc), panels, acc, (band + 2) % 4, ha.shape[1])


def rest_body(ha, hb, hc, panels, acc, near, mine):
    band = lax.axis_index("lat")
    partner = band + 1 - 2 * (band % 2)
    halo, cells = (ha, hb, hc), ha.shape[1]
    near[...] = band_sum(halo, panels, acc, partner, cells).astype(near.dtype)
    mine[...] = band_sum(halo, panels, acc, band, cells)


def pack_body(part, mine, other, out):
    width = out.shape[1]
    out[...] = (mine[:, part * width : (part + 1) * width] + other[...].astype(jnp.float32)).astype(out.dtype)


def final_body(mine, other, third, fourth, out):
    total = mine[...] + other[...].astype(jnp.float32)
    width = third.shape[1]
    for i, r in enumerate((third, fourth)):
        here = slice(i * width, (i + 1) * width)
        out[here, :] = (total[:, here] + r[...].astype(jnp.float32)).T


def sweep(residual, noise_weights, kernel):
    rows, columns, probes = residual.shape
    cells = rows * columns
    every = kernel.shape[3]
    f32, bf16 = jnp.float32, jnp.bfloat16
    shape = jax.ShapeDtypeStruct
    MB = 1 << 20

    weighted = call(
        weigh_body,
        pltpu.VMEM((probes, cells), bf16),
        [HBM] * 2,
        [
            pltpu.VMEM((rows, columns, probes), bf16),
            pltpu.VMEM((columns, rows), f32),
            pltpu.SemaphoreType.DMA((2,)),
        ],
        0,
        MB // 4,
        58 * MB,
    )(in_hbm(residual), in_hbm(noise_weights.T))
    halo = []
    for shifts in SHIFTS:
        halo.append(eastward(weighted, *shifts))
    ha, hb, hc = halo
    flops = 2 * probes * cells * every
    acc = call(
        first_body,
        shape((probes, every), f32),
        [VMEM, HBM],
        [pltpu.VMEM((cells, every), bf16), pltpu.SemaphoreType.DMA((4,))],
        flops,
        3 * MB,
        8 * MB,
    )(weighted, in_hbm(kernel))
    flops = 6 * probes * cells * cells
    half = shape((probes, cells // 2), bf16)
    others = []
    for i in range(2):
        far = call(functools.partial(far_body, i), half, [VMEM] * 5, [], flops // 2, MB, 8 * MB)(
            ha, hb, hc, kernel, acc
        )
        others.append(swapped(far, 1))
    own_far = call(own_far_body, shape((probes, cells), f32), [VMEM] * 5, [], flops, 2 * MB, 8 * MB)(
        ha, hb, hc, kernel, acc
    )
    thirds = []
    for i in range(2):
        packed = call(functools.partial(pack_body, i), half, [VMEM] * 2, [], 0, MB // 2, 4 * MB)(own_far, others[i])
        thirds.append(swapped(packed, 2))
    near, mine = call(
        rest_body,
        (shape((probes, cells), bf16), shape((probes, cells), f32)),
        [VMEM] * 5,
        [],
        2 * flops,
        4 * MB,
        8 * MB,
    )(ha, hb, hc, kernel, acc)
    other_near = swapped(near, 1)
    total = call(final_body, shape((cells, probes), f32), [VMEM] * 4, [], 0, MB, 4 * MB)(
        mine, other_near, *thirds
    )
    return total.reshape(1, rows, columns, probes)


def solution(mesh):
    return jax.shard_map(
        sweep,
        mesh=mesh,
        in_specs=(P("lat", "lon", None), P("lat", "lon"), P(None, None, "lat", None)),
        out_specs=P(None, "lat", "lon", None),
        check_vma=False,
    )
```

```python
import functools

import jax
import jax.numpy as jnp
from jax import lax
from jax.experimental import pallas as pl
from jax.experimental.pallas import tpu as pltpu
from jax.sharding import PartitionSpec as P


SHIFTS = ((3, 1), (1, 3), (2, 2))

VMEM = pl.BlockSpec(memory_space=pltpu.VMEM)
HBM = pl.BlockSpec(memory_space=pltpu.HBM)


def in_hbm(value):
    return pltpu.with_memory_space_constraint(value, pltpu.HBM)


def eastward(value, even, odd):
    length = lax.axis_size("lon")
    pairs = [(i, (i + (odd if i % 2 else even)) % length) for i in range(length)]
    return lax.ppermute(value, "lon", pairs)


def swapped(value, mask):
    length = lax.axis_size("lat")
    return lax.ppermute(value, "lat", [(i, i ^ mask) for i in range(length)])


def call(body, outs, in_specs, scratch, flops, nbytes, limit):
    return pl.pallas_call(
        body,
        out_shape=outs,
        in_specs=in_specs,
        out_specs=jax.tree.map(lambda _: VMEM, outs),
        scratch_shapes=scratch,
        cost_estimate=pl.CostEstimate(flops=flops, bytes_accessed=nbytes, transcendentals=0),
        compiler_params=pltpu.CompilerParams(vmem_limit_bytes=limit),
    )


def weigh_body(residual, noise, out, data, weights, sems):
    copies = [
        pltpu.make_async_copy(noise, weights, sems.at[0]),
        pltpu.make_async_copy(residual, data, sems.at[1]),
    ]
    for copy in copies:
        copy.start()
    for copy in copies:
        copy.wait()
    part = [
        (weights[:, y : y + 1] * data[y].astype(jnp.float32)).astype(out.dtype)
        for y in range(data.shape[0])
    ]
    out[...] = jnp.concatenate(part, axis=0).T


def first_body(weighted, panels, acc, own, sems):
    cells = weighted.shape[1]
    depth = cells // sems.shape[0]
    copies = [
        pltpu.make_async_copy(
            panels.at[0, 0, pl.ds(i * depth, depth)], own.at[pl.ds(i * depth, depth)], sems.at[i]
        )
        for i in range(sems.shape[0])
    ]
    for copy in copies:
        copy.start()
    for copy in copies:
        copy.wait()
    for k in range(panels.shape[3] // cells):
        where = slice(k * cells, (k + 1) * cells)
        acc[:, where] = jnp.dot(weighted[...], own[:, where], preferred_element_type=jnp.float32)


def band_sum(halo, panels, acc, band, cells, part=0, parts=1):
    width = cells // parts
    where = pl.ds(pl.multiple_of(band * cells + part * width, width), width)
    odd = lax.axis_index("lon") % 2
    total = acc[:, where]
    for (from_even, from_odd), h in zip(SHIFTS, halo):
        d = from_odd + (from_even - from_odd) * odd
        total += jnp.dot(h[...], panels[d, 0, :, where], preferred_element_type=jnp.float32)
    return total


def far_body(part, ha, hb, hc, panels, acc, out):
    band = 3 - lax.axis_index("lat")
    out[...] = band_sum((ha, hb, hc), panels, acc, band, ha.shape[1], part, 2).astype(out.dtype)


def own_far_body(ha, hb, hc, panels, acc, mine):
    band = lax.axis_index("lat")
    mine[...] = band_sum((ha, hb, hc), panels, acc, (band + 2) % 4, ha.shape[1])


def rest_body(ha, hb, hc, panels, acc, near, mine):
    band = lax.axis_index("lat")
    partner = band + 1 - 2 * (band % 2)
    halo, cells = (ha, hb, hc), ha.shape[1]
    near[...] = band_sum(halo, panels, acc, partner, cells).astype(near.dtype)
    mine[...] = band_sum(halo, panels, acc, band, cells)


def pack_body(part, mine, other, out):
    width = out.shape[1]
    out[...] = (mine[:, part * width : (part + 1) * width] + other[...].astype(jnp.float32)).astype(out.dtype)


def final_body(mine, other, third, fourth, out, rows, sems):
    width = third.shape[1]
    copies = []
    for i, r in enumerate((third, fourth)):
        here = slice(i * width, (i + 1) * width)
        total = mine[:, here] + other[:, here].astype(jnp.float32) + r[...].astype(jnp.float32)
        rows[here, :] = total.T
        part = pl.ds(i * width, width)
        copies.append(pltpu.make_async_copy(rows.at[part], out.at[part], sems.at[i]))
        copies[i].start()
    for copy in copies:
        copy.wait()


def sweep(residual, noise_weights, kernel):
    rows, columns, probes = residual.shape
    cells = rows * columns
    every = kernel.shape[3]
    f32, bf16 = jnp.float32, jnp.bfloat16
    shape = jax.ShapeDtypeStruct
    MB = 1 << 20

    weighted = call(
        weigh_body,
        pltpu.VMEM((probes, cells), bf16),
        [HBM] * 2,
        [
            pltpu.VMEM((rows, columns, probes), bf16),
            pltpu.VMEM((columns, rows), f32),
            pltpu.SemaphoreType.DMA((2,)),
        ],
        0,
        MB // 4,
        58 * MB,
    )(in_hbm(residual), in_hbm(noise_weights.T))
    halo = []
    for shifts in SHIFTS:
        halo.append(eastward(weighted, *shifts))
    ha, hb, hc = halo
    flops = 2 * probes * cells * every
    acc = call(
        first_body,
        shape((probes, every), f32),
        [VMEM, HBM],
        [pltpu.VMEM((cells, every), bf16), pltpu.SemaphoreType.DMA((4,))],
        flops,
        3 * MB,
        8 * MB,
    )(weighted, in_hbm(kernel))
    flops = 6 * probes * cells * cells
    half = shape((probes, cells // 2), bf16)
    others = []
    for i in range(2):
        far = call(functools.partial(far_body, i), half, [VMEM] * 5, [], flops // 2, MB, 8 * MB)(
            ha, hb, hc, kernel, acc
        )
        others.append(swapped(far, 1))
    own_far = call(own_far_body, shape((probes, cells), f32), [VMEM] * 5, [], flops, 2 * MB, 8 * MB)(
        ha, hb, hc, kernel, acc
    )
    thirds = []
    for i in range(2):
        packed = call(functools.partial(pack_body, i), half, [VMEM] * 2, [], 0, MB // 2, 4 * MB)(own_far, others[i])
        thirds.append(swapped(packed, 2))
    near, mine = call(
        rest_body,
        (shape((probes, cells), bf16), shape((probes, cells), f32)),
        [VMEM] * 5,
        [],
        2 * flops,
        4 * MB,
        8 * MB,
    )(ha, hb, hc, kernel, acc)
    other_near = swapped(near, 1)
    total = pl.pallas_call(
        final_body,
        out_shape=shape((cells, probes), f32),
        in_specs=[VMEM] * 4,
        out_specs=HBM,
        scratch_shapes=[pltpu.VMEM((cells, probes), f32), pltpu.SemaphoreType.DMA((2,))],
        compiler_params=pltpu.CompilerParams(vmem_limit_bytes=4 * MB),
    )(mine, other_near, *thirds)
    return total.reshape(1, rows, columns, probes)


def solution(mesh):
    return jax.shard_map(
        sweep,
        mesh=mesh,
        in_specs=(P("lat", "lon", None), P("lat", "lon"), P(None, None, "lat", None)),
        out_specs=P(None, "lat", "lon", None),
        check_vma=False,
    )
```
